32 devices in a mesh: spec: 16 (over z, y, x), wave: 2 (over core).
Axes of the slice: x: 2, y: 2, z: 4, core: 2. Of those that a mesh axis runs over, the one named last changes fastest.
Arguments:
- spectra_flux: bfloat16 [1024, 12288], P('spec', 'wave'), may hold values from 0.19921875 to 5
- pixel_offsets: int32 [1024], P('spec'), may hold values from 0 to 6143
- assignment: int32 [1024], P('spec'), may hold values from 0 to 127, as said below
- archetypes: bfloat16 [128, 12288], P('spec', 'wave'), may hold values from 0.19921875 to 5
- coefficients: float32 [1024, 12], P('spec'), may hold values from 0.1 to 1
- templates: float32 [12, 12288], P(None, 'wave'), may hold values from 0.1 to 1
Outputs:
- chi_square: float32 [1024, 128], P('spec', 'wave')
- archetype_update: float32 [128, 12288], P('spec', 'wave')
- final_coefficients: float32 [1024, 12], P('spec')
- final_templates: float32 [12, 12288], P(None, 'wave')
The draws below stay inside these ranges and needn't reach their ends.
Inputs may be any that keep to these rules, and one draw needn't show every extreme that they name: `assignment`: archetypes k * 8 to (k + 1) * 8 - 1 belong to owner k. The 64 spectra of one index of spec name one owner's archetypes at most 12 times, and one owner, the same on every index, is named exactly 12 times by each.
All inputs are finite; a program needn't handle non-finite values.
Results may differ from the reference program's by a relative error of at most 0.0014.
The reference program's roundings to bfloat16 on the way count: a program that leaves them out, or rounds other values in their place, can miss the bound.
Values may be sent and summed in bfloat16 or wider, within the bound.
No kernel may reach another device: no remote copies, remote signals or barrier semaphores. Data moves between devices by JAX's collectives and lax.ppermute only.
A program may use at most 64 MiB of HBM per device.

```python
import math
import jax
import jax.numpy as jnp
from jax import lax

PIXELS = 12288
COMPONENTS = 12
ARCH_DEV = 8
SPEC_DEV = 64
ITERATIONS = 4
SPECTRA = 1024
ARCHETYPES = 128
OWNER_SLOTS = 12


def draw_assignment(key, part):
    owners = SPECTRA // SPEC_DEV
    slot_count = owners * OWNER_SLOTS
    key_full, key_rows = jax.random.split(jax.random.fold_in(key, 7))
    full_owner = jax.random.randint(key_full, (), 0, owners)
    slot_owner = jnp.arange(slot_count, dtype=jnp.int32) // OWNER_SLOTS

    def one_block(block_key):
        key_perm, key_order, key_arch = jax.random.split(block_key, 3)
        noise = jax.random.permutation(key_perm, slot_count).astype(jnp.int32)
        score = jnp.where(slot_owner == full_owner, noise, noise + slot_count)
        order = jnp.argsort(score)
        picked = slot_owner[order[:SPEC_DEV]]
        shuffled = picked[jax.random.permutation(key_order, SPEC_DEV)]
        within = jax.random.randint(key_arch, (SPEC_DEV,), 0, ARCH_DEV)
        return shuffled * ARCH_DEV + within
    block_keys = jax.random.split(key_rows, owners)
    return jax.vmap(one_block)(block_keys).reshape(SPECTRA).astype(jnp.int32)


def with_ends(entries, key, smallest, top_value):
    longest = entries.shape.index(max(entries.shape))
    spots = []
    for shift in (0, 1):
        where = [jax.random.randint(jax.random.fold_in(key, axis), (), 0, length) for axis, length in enumerate(entries.shape)]
        where[longest] = (where[longest] + shift) % entries.shape[longest]
        spots.append(tuple(where))
    return entries.at[spots[0]].set(smallest).at[spots[1]].set(top_value)


def block_levels(key, shape, cuts, least, high):
    gain = 1.0
    for dim, parts in cuts:
        heights = jax.random.uniform(jax.random.fold_in(jax.random.fold_in(key, 6), dim), (parts,), jnp.float32, least / len(cuts), high / len(cuts))
        gain = gain * jnp.repeat(jnp.exp(heights), shape[dim] // parts).reshape((-1,) + (1,) * (len(shape) - 1 - dim))
    return gain


def setup_inputs(seed: int = 0) -> dict:
    keys = jax.random.split(jax.random.key(seed), 7)
    spectra_flux = jnp.clip(jnp.exp(math.log(5.0) - 3.2227897 * jax.random.uniform(keys[0], (SPECTRA, PIXELS), jnp.float32) ** block_levels(keys[0], (SPECTRA, PIXELS), ((0, 16), (1, 2)), -0.2, 0.2)), 0.19921875, 5.0).astype(jnp.bfloat16)
    pixel_offsets = with_ends(jax.random.randint(keys[1], (SPECTRA,), 0, PIXELS // 2), jax.random.fold_in(keys[1], 1), 0, (PIXELS // 2) - 1).astype(jnp.int32)
    assignment = draw_assignment(jax.random.fold_in(keys[6], 71), 0)
    archetypes = jnp.clip(jnp.exp(math.log(5.0) - 3.2227897 * jax.random.uniform(keys[3], (ARCHETYPES, PIXELS), jnp.float32) ** block_levels(keys[3], (ARCHETYPES, PIXELS), ((0, 16), (1, 2)), -0.2, 0.2)), 0.19921875, 5.0).astype(jnp.bfloat16)
    coefficients = jnp.clip(jnp.exp(math.log(1.0) - 2.3025851 * jax.random.uniform(keys[4], (SPECTRA, COMPONENTS), jnp.float32) ** block_levels(keys[4], (SPECTRA, COMPONENTS), ((0, 16),), -0.2, 0.2)), 0.1, 1.0)
    templates = jnp.clip(jnp.exp(math.log(1.0) - 2.3025851 * jax.random.uniform(keys[5], (COMPONENTS, PIXELS), jnp.float32) ** block_levels(keys[5], (COMPONENTS, PIXELS), ((1, 2),), -0.2, 0.2)), 0.1, 1.0)
    return {"spectra_flux": spectra_flux, "pixel_offsets": pixel_offsets, "assignment": assignment, "archetypes": archetypes, "coefficients": coefficients, "templates": templates}


def reference(spectra_flux, pixel_offsets, assignment, archetypes, coefficients, templates):
    blocks = SPECTRA // SPEC_DEV
    pixel_index = jnp.arange(PIXELS, dtype=jnp.int32)
    arch_float = archetypes.astype(jnp.float32)
    arch_square = lax.optimization_barrier((arch_float * arch_float).astype(jnp.bfloat16)).astype(jnp.float32)
    flux_blocks = spectra_flux.reshape(blocks, SPEC_DEV, PIXELS)
    offset_blocks = pixel_offsets.reshape(blocks, SPEC_DEV)
    assign_blocks = assignment.reshape(blocks, SPEC_DEV)

    def fit_block(carry, inputs):
        flux_rows, offset_rows, assign_rows = inputs
        mask_rows = (pixel_index[None, :] >= offset_rows[:, None]).astype(jnp.float32)
        flux_float = flux_rows.astype(jnp.float32)
        masked_rows = flux_float * mask_rows
        cross = jnp.dot(masked_rows, arch_float.T, precision=lax.Precision.HIGHEST)
        normal = jnp.dot(mask_rows, arch_square.T, precision=lax.Precision.HIGHEST)
        energy = jnp.sum(masked_rows * masked_rows, axis=1)
        valid = (PIXELS - offset_rows).astype(jnp.float32)
        chi_rows = (energy[:, None] - cross * cross / normal) / valid[:, None]
        pick_index = assign_rows[:, None].astype(jnp.int32)
        cross_pick = jnp.take_along_axis(cross, pick_index, axis=1)[:, 0]
        norm_pick = jnp.take_along_axis(normal, pick_index, axis=1)[:, 0]
        scale_fit = cross_pick / norm_pick
        chosen = arch_float[assign_rows]
        residual = (mask_rows * (flux_float - scale_fit[:, None] * chosen)).astype(jnp.bfloat16)
        residual = lax.optimization_barrier(residual).astype(jnp.float32)
        sums, counts = carry
        sums = sums + jax.ops.segment_sum(residual, assign_rows, num_segments=ARCHETYPES)
        counts = counts + jax.ops.segment_sum(jnp.ones((SPEC_DEV,), jnp.float32), assign_rows, num_segments=ARCHETYPES)
        return (sums, counts), chi_rows

    start_carry = (jnp.zeros((ARCHETYPES, PIXELS), jnp.float32), jnp.zeros((ARCHETYPES,), jnp.float32))
    (sums, counts), chi_blocks = lax.scan(fit_block, start_carry, (flux_blocks, offset_blocks, assign_blocks))
    chi_square = chi_blocks.reshape(SPECTRA, ARCHETYPES)
    archetype_update = sums / (counts[:, None] + 1.0)

    mask_all = (pixel_index[None, :] >= pixel_offsets[:, None]).astype(jnp.bfloat16)
    masked_all = (spectra_flux * mask_all).reshape(blocks, SPEC_DEV, PIXELS)
    weights = coefficients
    basis = templates
    for iteration in range(ITERATIONS):
        basis_half = lax.optimization_barrier(basis.astype(jnp.bfloat16)).astype(jnp.float32)

        def coef_block(rows_block):
            return jnp.dot(rows_block.astype(jnp.float32), basis_half.T, precision=lax.Precision.HIGHEST)

        numer_coef = lax.map(coef_block, masked_all).reshape(SPECTRA, COMPONENTS)
        gram = jnp.dot(basis, basis.T, precision=lax.Precision.HIGHEST)
        weights = weights * numer_coef / jnp.dot(weights, gram, precision=lax.Precision.HIGHEST)
        weights_half = lax.optimization_barrier(weights.astype(jnp.bfloat16)).astype(jnp.float32)
        weight_blocks = weights_half.reshape(blocks, SPEC_DEV, COMPONENTS)

        def basis_block(total, pair):
            return total + jnp.dot(pair[0].T, pair[1].astype(jnp.float32), precision=lax.Precision.HIGHEST), None

        numer_basis, unused = lax.scan(basis_block, jnp.zeros((COMPONENTS, PIXELS), jnp.float32), (weight_blocks, masked_all))
        cross_gram = jnp.dot(weights.T, weights, precision=lax.Precision.HIGHEST)
        basis = basis * numer_basis / jnp.dot(cross_gram, basis, precision=lax.Precision.HIGHEST)
    return (chi_square, archetype_update, weights, basis)
```

```python
import jax
import jax.numpy as jnp
from jax import lax
from jax.sharding import PartitionSpec as P

ITERATIONS = 4
HIGHEST = lax.Precision.HIGHEST
ALL = ("spec", "wave")


def stages(count):
    found, bit = [(1,)], 2
    while bit < count:
        if bit * 2 < count:
            found.append((bit, bit * 2, bit * 3))
            bit *= 4
        else:
            found.append((bit,))
            bit *= 2
    return found


def all_sum(part, count):
    for masks in stages(count):
        others = [
            lax.ppermute(part, ALL, [(i, i ^ mask) for i in range(count)]) for mask in masks
        ]
        for other in others:
            part = part + other
    return part


def dot_rows(left, right, **kwargs):
    return lax.dot_general(left, right, (((1,), (1,)), ((), ())), **kwargs)


def spread(block, parts):
    return jnp.broadcast_to(block[None], (parts,) + block.shape)


def on_device(spectra_flux, pixel_offsets, assignment, archetypes, coefficients, templates):
    rows, pixels = spectra_flux.shape
    arch_own = archetypes.shape[0]
    comps = templates.shape[0]
    spec_count, wave_count = lax.axis_size("spec"), lax.axis_size("wave")
    total = spec_count * wave_count
    spectra, arches = rows * spec_count, arch_own * spec_count
    strip = pixels // spec_count
    spec_at, wave_at = lax.axis_index("spec"), lax.axis_index("wave")

    pixel_index = wave_at * pixels + jnp.arange(pixels, dtype=jnp.int32)
    mask_rows = (pixel_index[None, :] >= pixel_offsets[:, None]).astype(jnp.bfloat16)
    masked_rows = spectra_flux * mask_rows
    both = jnp.concatenate([masked_rows, archetypes], axis=0)
    both = both.reshape(rows + arch_own, spec_count, strip).swapaxes(0, 1)
    both = lax.all_to_all(both, "spec", 0, 0, tiled=True)
    masked = both[:, :rows].reshape(spectra, strip)
    arch = both[:, rows:].reshape(arches, strip)

    numer_part = dot_rows(
        masked_rows, templates.astype(jnp.bfloat16), preferred_element_type=jnp.float32
    )
    gram_part = dot_rows(templates, templates, precision=HIGHEST)
    numer, gram = lax.psum((numer_part, gram_part), "wave")
    first = coefficients * numer / jnp.dot(coefficients, gram, precision=HIGHEST)
    facts = jnp.concatenate(
        [
            first.T,
            pixel_offsets.astype(jnp.float32)[None],
            assignment.astype(jnp.float32)[None],
        ],
        axis=0,
    )
    facts = lax.all_to_all(spread(facts, spec_count), "spec", 0, 0, tiled=True)
    facts = facts.reshape(spec_count, comps + 2, rows).swapaxes(0, 1).reshape(comps + 2, spectra)
    weights = facts[:comps]
    offsets = facts[comps].astype(jnp.int32)
    named = facts[comps + 1].astype(jnp.int32)

    strip_index = wave_at * pixels + spec_at * strip + jnp.arange(strip, dtype=jnp.int32)
    mask = (strip_index[None, :] >= offsets[:, None]).astype(jnp.bfloat16)
    hot = named[:, None] == jnp.arange(arches, dtype=jnp.int32)[None, :]
    hot_half = hot.astype(jnp.bfloat16)
    arch_float = arch.astype(jnp.float32)
    squares = (arch_float * arch_float).astype(jnp.bfloat16)
    cross_part = dot_rows(masked, arch, preferred_element_type=jnp.float32)
    normal_part = dot_rows(mask, squares, preferred_element_type=jnp.float32)
    masked_float = masked.astype(jnp.float32)
    energy_part = jnp.sum(masked_float * masked_float, axis=1)
    cross_pick = jnp.sum(jnp.where(hot, cross_part, 0.0), axis=1)
    normal_pick = jnp.sum(jnp.where(hot, normal_part, 0.0), axis=1)

    basis = lax.dynamic_slice_in_dim(templates, spec_at * strip, strip, 1)
    for iteration in range(ITERATIONS):
        if iteration:
            numer_part = dot_rows(
                basis.astype(jnp.bfloat16), masked, preferred_element_type=jnp.float32
            )
            gram_part = dot_rows(basis, basis, precision=HIGHEST)
            parts = [numer_part, gram_part]
            if iteration == 1:
                picks = jnp.stack([cross_pick, normal_pick, energy_part])
                parts = [jnp.concatenate([numer_part, picks], axis=0), jnp.pad(gram_part, ((0, 3), (0, 0)))]
            whole = all_sum(jnp.concatenate(parts, axis=1), total)
            if iteration == 1:
                cross_pick, normal_pick, energy = (whole[comps + i, :spectra] for i in range(3))
            gram = whole[:comps, spectra:]
            weights = weights * whole[:comps, :spectra] / jnp.dot(gram, weights, precision=HIGHEST)
        numer_basis = jnp.dot(
            weights.astype(jnp.bfloat16), masked, preferred_element_type=jnp.float32
        )
        cross_gram = dot_rows(weights, weights, precision=HIGHEST)
        basis = basis * numer_basis / jnp.dot(cross_gram, basis, precision=HIGHEST)

    own = lax.dynamic_slice_in_dim(weights, spec_at * rows, rows, 1)
    full = lax.all_to_all(spread(basis, spec_count), "spec", 0, 0, tiled=True)
    full = full.reshape(spec_count, comps, strip).swapaxes(0, 1).reshape(comps, pixels)

    share = arches // wave_count
    pair = jnp.stack([cross_part, normal_part])
    pair = pair.reshape(2, spectra, wave_count, share).transpose(2, 0, 1, 3)
    pair = lax.all_to_all(pair, "wave", 0, 0, tiled=True).reshape(wave_count, 2, spectra, share).sum(0)
    pair = pair.reshape(2, spec_count, rows, share).swapaxes(0, 1)
    pair = lax.all_to_all(pair, "spec", 0, 0, tiled=True).sum(0)
    energy_own = lax.dynamic_slice_in_dim(energy, spec_at * rows, rows, 0)
    valid = (pixels * wave_count - pixel_offsets).astype(jnp.float32)
    chi_square = (energy_own[:, None] - pair[0] * pair[0] / pair[1]) / valid[:, None]

    scale_fit = cross_pick / normal_pick
    chosen = jnp.dot(hot_half, arch, preferred_element_type=jnp.float32)
    residual = (masked_float - mask.astype(jnp.float32) * (scale_fit[:, None] * chosen)).astype(
        jnp.bfloat16
    )
    sums = lax.dot_general(
        hot_half, residual, (((0,), (0,)), ((), ())), preferred_element_type=jnp.float32
    )
    counts = jnp.sum(hot.astype(jnp.float32), axis=0)
    update = sums / (counts[:, None] + 1.0)
    update = lax.all_to_all(update, "spec", 0, 0, tiled=True)
    update = update.reshape(spec_count, arch_own, strip).swapaxes(0, 1).reshape(arch_own, pixels)
    return (chi_square, update, own.T, full)


def solution(mesh):
    placed = (
        P("spec", "wave"),
        P("spec"),
        P("spec"),
        P("spec", "wave"),
        P("spec", None),
        P(None, "wave"),
    )
    return jax.shard_map(
        on_device,
        mesh=mesh,
        in_specs=placed,
        out_specs=(P("spec", "wave"), P("spec", "wave"), P("spec", None), P(None, "wave")),
        check_vma=False,
    )
```

```python
import jax
import jax.numpy as jnp
from jax import lax
from jax.sharding import PartitionSpec as P

ITERATIONS = 4
HIGHEST = lax.Precision.HIGHEST
ALL = ("spec", "wave")


def swap(part, mask, count):
    return lax.ppermute(part, ALL, [(i, i ^ mask) for i in range(count)])


def stages(first, count):
    found, bit = [], first
    while bit < count:
        if bit * 2 < count:
            found.append((bit, bit * 2, bit * 3))
            bit *= 4
        else:
            found.append((bit,))
            bit *= 2
    return found


def all_sum(part, place, count):
    odd = jnp.bitwise_and(place, 1)
    half = part.shape[0] // 2
    mine = lax.dynamic_slice_in_dim(part, odd * half, half, 0)
    theirs = lax.dynamic_slice_in_dim(part, (1 - odd) * half, half, 0)
    mine = mine + swap(theirs, 1, count)
    for masks in stages(2, count):
        others = [swap(mine, mask, count) for mask in masks]
        for other in others:
            mine = mine + other
    other = swap(mine, 1, count)
    return jnp.concatenate(
        [jnp.where(odd == 0, mine, other), jnp.where(odd == 0, other, mine)], axis=0
    )


def gather_columns(block, first, place, count):
    for masks in stages(first, count):
        blocks = [block] + [swap(block, mask, count) for mask in masks]
        for step, mask in enumerate(masks[:2]):
            bit = jnp.bitwise_and(place, mask)
            stride = 1 << step
            blocks = [
                jnp.where(bit != 0, blocks[i ^ stride], blocks[i]) for i in range(len(blocks))
            ]
        block = jnp.concatenate(blocks, axis=1)
    return block


def dot_rows(left, right, **kwargs):
    return lax.dot_general(left, right, (((1,), (1,)), ((), ())), **kwargs)


def spread(block, parts):
    return jnp.broadcast_to(block[None], (parts,) + block.shape)


def on_device(spectra_flux, pixel_offsets, assignment, archetypes, coefficients, templates):
    rows, pixels = spectra_flux.shape
    arch_own = archetypes.shape[0]
    comps = templates.shape[0]
    spec_count, wave_count = lax.axis_size("spec"), lax.axis_size("wave")
    total = spec_count * wave_count
    spectra, arches = rows * spec_count, arch_own * spec_count
    strip = pixels // spec_count
    spec_at, wave_at = lax.axis_index("spec"), lax.axis_index("wave")
    place = spec_at * wave_count + wave_at
    share = arches // wave_count

    pixel_index = wave_at * pixels + jnp.arange(pixels, dtype=jnp.int32)
    mask_rows = (pixel_index[None, :] >= pixel_offsets[:, None]).astype(jnp.bfloat16)
    masked_rows = spectra_flux * mask_rows
    both = jnp.concatenate([masked_rows, archetypes], axis=0)
    both = both.reshape(rows + arch_own, spec_count, strip).swapaxes(0, 1)
    both = lax.all_to_all(both, "spec", 0, 0, tiled=True)
    masked = both[:, :rows].reshape(spectra, strip)
    arch = both[:, rows:].reshape(arches, strip)

    numer_part = dot_rows(
        masked_rows, templates.astype(jnp.bfloat16), preferred_element_type=jnp.float32
    )
    gram_part = dot_rows(templates, templates, precision=HIGHEST)
    numer, gram = lax.psum((numer_part, gram_part), "wave")
    first = coefficients * numer / jnp.dot(coefficients, gram, precision=HIGHEST)
    facts = jnp.concatenate(
        [
            first.T,
            pixel_offsets.astype(jnp.float32)[None],
            assignment.astype(jnp.float32)[None],
        ],
        axis=0,
    )
    facts = gather_columns(facts, wave_count, place, total)
    weights = facts[:comps]
    offsets = facts[comps].astype(jnp.int32)
    named = facts[comps + 1].astype(jnp.int32)

    strip_index = wave_at * pixels + spec_at * strip + jnp.arange(strip, dtype=jnp.int32)
    mask = (strip_index[None, :] >= offsets[:, None]).astype(jnp.bfloat16)
    hot = named[:, None] == jnp.arange(arches, dtype=jnp.int32)[None, :]
    hot_half = hot.astype(jnp.bfloat16)
    arch_float = arch.astype(jnp.float32)
    squares = (arch_float * arch_float).astype(jnp.bfloat16)
    masked_float = masked.astype(jnp.float32)
    energy_part = jnp.sum(masked_float * masked_float, axis=1)
    arch_parts = arch.reshape(wave_count, share, strip)
    square_parts = squares.reshape(wave_count, share, strip)
    blank = jnp.zeros_like(arch_parts)
    right = jnp.concatenate(
        [
            jnp.concatenate([arch_parts, blank], axis=2),
            jnp.concatenate([blank, square_parts], axis=2),
        ],
        axis=1,
    ).reshape(2 * arches, 2 * strip)
    pair_part = dot_rows(
        jnp.concatenate([masked, mask], axis=1), right, preferred_element_type=jnp.float32
    )
    column = jnp.arange(2 * arches, dtype=jnp.int32)[None, :]
    cross_column = (named // share * (2 * share) + named % share)[:, None]
    cross_pick = jnp.sum(jnp.where(column == cross_column, pair_part, 0.0), axis=1)
    normal_pick = jnp.sum(jnp.where(column == cross_column + share, pair_part, 0.0), axis=1)
    pair = lax.dynamic_slice_in_dim(pair_part, wave_at * 2 * share, 2 * share, 1)
    for mask_bits in range(1, wave_count):
        sent = (wave_at ^ mask_bits) * 2 * share
        pair = pair + swap(
            lax.dynamic_slice_in_dim(pair_part, sent, 2 * share, 1), mask_bits, total
        )
    pair = pair.reshape(spec_count, rows, 2 * share)
    pair = lax.all_to_all(pair, "spec", 0, 0, tiled=True).sum(0)

    basis = lax.dynamic_slice_in_dim(templates, spec_at * strip, strip, 1)
    for iteration in range(ITERATIONS):
        if iteration:
            numer_part = dot_rows(
                basis.astype(jnp.bfloat16), masked, preferred_element_type=jnp.float32
            )
            gram_part = dot_rows(basis, basis, precision=HIGHEST)
            part = jnp.concatenate([numer_part, jnp.pad(gram_part, ((0, 0), (0, 128 - comps)))], axis=1)
            extra = jnp.zeros((16 - comps, spectra + 128), jnp.float32)
            if iteration == 1:
                extra = jnp.pad(jnp.stack([cross_pick, normal_pick, energy_part]), ((0, 13 - comps), (0, 128)))
            whole = all_sum(jnp.concatenate([part, extra], axis=0), place, total)
            if iteration == 1:
                cross_pick, normal_pick, energy = (whole[comps + i, :spectra] for i in range(3))
            gram = whole[:comps, spectra : spectra + comps]
            weights = weights * whole[:comps, :spectra] / jnp.dot(gram, weights, precision=HIGHEST)
        numer_basis = jnp.dot(
            weights.astype(jnp.bfloat16), masked, preferred_element_type=jnp.float32
        )
        cross_gram = dot_rows(weights, weights, precision=HIGHEST)
        basis = basis * numer_basis / jnp.dot(cross_gram, basis, precision=HIGHEST)

    own = lax.dynamic_slice_in_dim(weights, spec_at * rows, rows, 1)
    full = lax.all_to_all(spread(basis, spec_count), "spec", 0, 0, tiled=True)
    full = full.reshape(spec_count, comps, strip).swapaxes(0, 1).reshape(comps, pixels)

    energy_own = lax.dynamic_slice_in_dim(energy, spec_at * rows, rows, 0)
    valid = (pixels * wave_count - pixel_offsets).astype(jnp.float32)
    chi_square = (energy_own[:, None] - pair[:, :share] * pair[:, :share] / pair[:, share:]) / valid[:, None]

    scale_fit = cross_pick / normal_pick
    chosen = jnp.dot(hot_half, arch, preferred_element_type=jnp.float32)
    residual = (masked_float - mask.astype(jnp.float32) * (scale_fit[:, None] * chosen)).astype(
        jnp.bfloat16
    )
    sums = lax.dot_general(
        hot_half, residual, (((0,), (0,)), ((), ())), preferred_element_type=jnp.float32
    )
    counts = jnp.sum(hot.astype(jnp.float32), axis=0)
    update = sums / (counts[:, None] + 1.0)
    update = lax.all_to_all(update, "spec", 0, 0, tiled=True)
    update = update.reshape(spec_count, arch_own, strip).swapaxes(0, 1).reshape(arch_own, pixels)
    return (chi_square, update, own.T, full)


def solution(mesh):
    placed = (
        P("spec", "wave"),
        P("spec"),
        P("spec"),
        P("spec", "wave"),
        P("spec", None),
        P(None, "wave"),
    )
    return jax.shard_map(
        on_device,
        mesh=mesh,
        in_specs=placed,
        out_specs=(P("spec", "wave"), P("spec", "wave"), P("spec", None), P(None, "wave")),
        check_vma=False,
    )
```

```python
import functools

import jax
import jax.numpy as jnp
from jax import lax
from jax.experimental import pallas as pl
from jax.experimental.pallas import tpu as pltpu
from jax.sharding import PartitionSpec as P

ITERATIONS = 4
HIGHEST = lax.Precision.HIGHEST
ALL = ("spec", "wave")
LANES = 128
HALF = 8


def swap(part, mask, count):
    return lax.ppermute(part, ALL, [(i, i ^ mask) for i in range(count)])


def stages(first, count):
    found, bit = [], first
    while bit < count:
        if bit * 2 < count:
            found.append((bit, bit * 2, bit * 3))
            bit *= 4
        else:
            found.append((bit,))
            bit *= 2
    return found


def all_sum(mine, theirs, count, beside=None):
    mine = mine + swap(theirs, 1, count)
    groups = stages(2, count)
    for at, masks in enumerate(groups):
        others = [swap(mine, mask, count) for mask in masks]
        for other in others:
            mine = mine + other
        if at == 0 and beside is not None:
            mine, beside = lax.optimization_barrier((mine, beside))
    return mine, swap(mine, 1, count), beside


def dot_rows(left, right, **kwargs):
    return lax.dot_general(left, right, (((1,), (1,)), ((), ())), **kwargs)


def spread(block, parts):
    return jnp.broadcast_to(block[None], (parts,) + block.shape)


def half_parts(value):
    parts = []
    for _ in range(3):
        part = lax.reduce_precision(value, 8, 7)
        parts.append(part.astype(jnp.bfloat16))
        value = value - part
    return parts


def place_is_odd():
    place = lax.axis_index("spec") * lax.axis_size("wave") + lax.axis_index("wave")
    return jnp.bitwise_and(place, 1) == 1


def update_basis(weights, basis, masked):
    numer = jnp.dot(weights.astype(jnp.bfloat16), masked, preferred_element_type=jnp.float32)
    cross_gram = dot_rows(weights, weights, precision=HIGHEST, preferred_element_type=jnp.float32)
    lower = jnp.dot(cross_gram, basis, precision=HIGHEST, preferred_element_type=jnp.float32)
    return basis * numer / lower


def store_halves(mine_ref, theirs_ref, numer, gram, extra):
    comps, spectra = numer.shape
    odd = place_is_odd()
    low, high = numer[:HALF], jnp.concatenate([numer[HALF:], extra], axis=0)
    mine_ref[:, :spectra] = jnp.where(odd, high, low)
    theirs_ref[:, :spectra] = jnp.where(odd, low, high)
    wide = jnp.concatenate([gram, jnp.zeros((comps, LANES - comps), jnp.float32)], axis=1)
    wide = jnp.concatenate([wide, jnp.zeros((2 * HALF - comps, LANES), jnp.float32)], axis=0)
    mine_ref[:, spectra:] = jnp.where(odd, wide[HALF:], wide[:HALF])
    theirs_ref[:, spectra:] = jnp.where(odd, wide[:HALF], wide[HALF:])


def load_masked(got_ref, rows):
    count, _, strip = got_ref.shape
    return got_ref[:, :rows, :].reshape(count * rows, strip)


def next_terms(basis, masked):
    numer = dot_rows(basis.astype(jnp.bfloat16), masked, preferred_element_type=jnp.float32)
    gram = dot_rows(basis, basis, precision=HIGHEST, preferred_element_type=jnp.float32)
    return numer, gram


def open_kernel(rows, own, got_ref, weights_ref, basis_ref, named_ref, basis_out, mine_ref, theirs_ref):
    masked = load_masked(got_ref, rows)
    count, _, strip = got_ref.shape
    basis = update_basis(weights_ref[...], basis_ref[...], masked)
    basis_out[...] = basis
    numer, gram = next_terms(basis, masked)
    arch = got_ref[:, rows : rows + own, :].astype(jnp.float32).reshape(count * own, strip)
    squares = (arch * arch).astype(jnp.bfloat16)
    mask = jnp.where(masked.astype(jnp.float32) != 0.0, 1.0, 0.0).astype(jnp.bfloat16)
    spectra = count * rows
    hot = lax.broadcasted_iota(jnp.int32, (count * own, spectra), 0) == named_ref[...]
    cross = dot_rows(arch.astype(jnp.bfloat16), masked, preferred_element_type=jnp.float32)
    normal = dot_rows(squares, mask, preferred_element_type=jnp.float32)
    cross = jnp.sum(jnp.where(hot, cross, 0.0), axis=0, keepdims=True)
    normal = jnp.sum(jnp.where(hot, normal, 0.0), axis=0, keepdims=True)
    power = masked.astype(jnp.float32) * masked.astype(jnp.float32)
    high = power.astype(jnp.bfloat16)
    low = (power - high.astype(jnp.float32)).astype(jnp.bfloat16)
    ones = jnp.ones((HALF, strip), jnp.bfloat16)
    energy = dot_rows(ones, high, preferred_element_type=jnp.float32) + dot_rows(
        ones, low, preferred_element_type=jnp.float32
    )
    blank = jnp.zeros((2 * HALF - numer.shape[0] - 3, spectra), jnp.float32)
    extra = jnp.concatenate([cross, normal, energy[:1], blank], axis=0)
    store_halves(mine_ref, theirs_ref, numer, gram, extra)


def step_kernel(rows, last, mine_in, other_in, weights_ref, basis_ref, got_ref, weights_out, basis_out, *halves):
    odd = place_is_odd()
    comps, spectra = weights_ref.shape
    low = jnp.where(odd, other_in[...], mine_in[...])
    high = jnp.where(odd, mine_in[...], other_in[...])
    both = jnp.concatenate([low, high], axis=0)[:comps]
    gram = both[:, spectra : spectra + comps]
    weights = weights_ref[...]
    lower = jnp.dot(gram, weights, precision=HIGHEST, preferred_element_type=jnp.float32)
    weights = weights * both[:, :spectra] / lower
    weights_out[...] = weights
    masked = load_masked(got_ref, rows)
    basis = update_basis(weights, basis_ref[...], masked)
    if last:
        for at in range(basis_out.shape[0]):
            basis_out[at] = basis
        return
    basis_out[...] = basis
    numer, gram = next_terms(basis, masked)
    blank = jnp.zeros((2 * HALF - comps, spectra), jnp.float32)
    store_halves(*halves, numer, gram, blank)


def line_kernel(blocks_ref, line_ref):
    count, _, strip = blocks_ref.shape
    for at in range(count):
        line_ref[:, at * strip : (at + 1) * strip] = blocks_ref[at]


def call(kernel, outs):
    return pl.pallas_call(kernel, out_shape=[jax.ShapeDtypeStruct(shape, jnp.float32) for shape in outs])


def on_device(spectra_flux, pixel_offsets, assignment, archetypes, coefficients, templates):
    rows, pixels = spectra_flux.shape
    own = archetypes.shape[0]
    comps = templates.shape[0]
    spec_count, wave_count = lax.axis_size("spec"), lax.axis_size("wave")
    total = spec_count * wave_count
    spectra, arches = rows * spec_count, own * spec_count
    strip = pixels // spec_count
    share = arches // wave_count
    spec_at, wave_at = lax.axis_index("spec"), lax.axis_index("wave")
    table = (HALF, spectra + LANES)

    pixel_index = wave_at * pixels + jnp.arange(pixels, dtype=jnp.int32)
    mask_rows = (pixel_index[None, :] >= pixel_offsets[:, None]).astype(jnp.bfloat16)
    masked_rows = spectra_flux * mask_rows
    numer = dot_rows(templates.astype(jnp.bfloat16), masked_rows, preferred_element_type=jnp.float32)
    gram = dot_rows(templates, templates, precision=HIGHEST)
    sums = jnp.concatenate([numer, gram], axis=1)
    part = sums
    for mask_bits in range(1, wave_count):
        sums = sums + swap(part, mask_bits, total)
    begun = coefficients.T
    first = begun * sums[:, :rows] / jnp.dot(sums[:, rows:], begun, precision=HIGHEST)

    high, middle, low = half_parts(first)
    ids = jnp.stack([assignment // LANES, assignment % LANES]).astype(jnp.bfloat16)
    facts = jnp.concatenate([high, ids, middle, low], axis=0)
    lines = facts.shape[0]
    fact_rows = pl.cdiv(pl.cdiv(lines * rows, strip), 8) * 8
    facts = jnp.pad(facts.reshape(-1), (0, fact_rows * strip - lines * rows)).reshape(fact_rows, strip)
    moved = jnp.concatenate([masked_rows, archetypes], axis=0)
    moved = moved.reshape(rows + own, spec_count, strip).swapaxes(0, 1)
    moved = jnp.concatenate([moved, spread(facts, spec_count)], axis=1)
    got = lax.all_to_all(moved, "spec", 0, 0, tiled=True)
    facts = got[:, rows + own :].reshape(spec_count, -1)[:, : lines * rows].astype(jnp.float32)
    facts = facts.reshape(spec_count, lines, rows).swapaxes(0, 1).reshape(lines, spectra)
    weights = facts[:comps] + (facts[comps + 2 : 2 * comps + 2] + facts[2 * comps + 2 :])
    named = (facts[comps] * LANES + facts[comps + 1]).astype(jnp.int32)

    basis = lax.dynamic_slice_in_dim(templates, spec_at * strip, strip, 1)
    basis, mine, theirs = call(
        functools.partial(open_kernel, rows, own), [(comps, strip), table, table]
    )(got, weights, basis, named[None])

    masked = got[:, :rows].reshape(spectra, strip)
    arch = got[:, rows : rows + own].reshape(arches, strip)
    mask = jnp.where(masked != 0, 1, 0).astype(jnp.bfloat16)
    arch_float = arch.astype(jnp.float32)
    squares = (arch_float * arch_float).astype(jnp.bfloat16)
    arch_parts = arch.reshape(wave_count, share, strip)
    square_parts = squares.reshape(wave_count, share, strip)
    blank = jnp.zeros_like(arch_parts)
    right = jnp.concatenate(
        [
            jnp.concatenate([arch_parts, blank], axis=2),
            jnp.concatenate([blank, square_parts], axis=2),
        ],
        axis=1,
    ).reshape(2 * arches, 2 * strip)
    pair_part = dot_rows(
        jnp.concatenate([masked, mask], axis=1), right, preferred_element_type=jnp.float32
    )
    pair = lax.dynamic_slice_in_dim(pair_part, wave_at * 2 * share, 2 * share, 1)
    for mask_bits in range(1, wave_count):
        sent = (wave_at ^ mask_bits) * 2 * share
        pair = pair + swap(
            lax.dynamic_slice_in_dim(pair_part, sent, 2 * share, 1), mask_bits, total
        )

    mine, other, pair = all_sum(mine, theirs, total, pair)
    pair = pair.reshape(spec_count, rows, 2 * share)
    pair = lax.all_to_all(pair, "spec", 0, 0, tiled=True)
    odd = place_is_odd()
    extra = jnp.where(odd, mine, other)
    at = comps - HALF
    scale_fit = extra[at, :spectra] / extra[at + 1, :spectra]
    energy = lax.dynamic_slice_in_dim(extra[at + 2], spec_at * rows, rows, 0)
    weights, basis, mine, theirs = call(
        functools.partial(step_kernel, rows, False), [(comps, spectra), (comps, strip), table, table]
    )(mine, other, weights, basis, got)

    hot = named[:, None] == jnp.arange(arches, dtype=jnp.int32)[None, :]
    hot_half = hot.astype(jnp.bfloat16)
    chosen = jnp.dot(hot_half, arch, preferred_element_type=jnp.float32)
    residual = (
        masked.astype(jnp.float32) - mask.astype(jnp.float32) * (scale_fit[:, None] * chosen)
    ).astype(jnp.bfloat16)
    sums = lax.dot_general(
        hot_half, residual, (((0,), (0,)), ((), ())), preferred_element_type=jnp.float32
    )
    counts = jnp.sum(hot.astype(jnp.float32), axis=0)
    update = sums / (counts[:, None] + 1.0)

    for iteration in range(2, ITERATIONS):
        beside = pair if iteration == 2 else update
        mine, other, beside = all_sum(mine, theirs, total, beside)
        if iteration == 2:
            pair = beside
            update, pair = lax.optimization_barrier((update, pair))
            update = lax.all_to_all(update, "spec", 0, 0, tiled=True)
        else:
            update = beside
        last = iteration == ITERATIONS - 1
        outs = [(comps, spectra)]
        outs += [(spec_count, comps, strip)] if last else [(comps, strip), table, table]
        weights, basis, *halves = call(functools.partial(step_kernel, rows, last), outs)(
            mine, other, weights, basis, got
        )
        if not last:
            mine, theirs = halves

    own_weights = lax.dynamic_slice_in_dim(weights, spec_at * rows, rows, 1)
    full = lax.all_to_all(basis, "spec", 0, 0, tiled=True)
    (full,) = call(line_kernel, [(comps, pixels)])(full)

    pair = pair.sum(0)
    valid = (pixels * wave_count - pixel_offsets).astype(jnp.float32)
    chi_square = (energy[:, None] - pair[:, :share] * pair[:, :share] / pair[:, share:]) / valid[:, None]
    (update,) = call(line_kernel, [(own, pixels)])(update.reshape(spec_count, own, strip))
    return (chi_square, update, own_weights.T, full)


def solution(mesh):
    placed = (
        P("spec", "wave"),
        P("spec"),
        P("spec"),
        P("spec", "wave"),
        P("spec", None),
        P(None, "wave"),
    )
    return jax.shard_map(
        on_device,
        mesh=mesh,
        in_specs=placed,
        out_specs=(P("spec", "wave"), P("spec", "wave"), P("spec", None), P(None, "wave")),
        check_vma=False,
    )
```

```python
import functools

import jax
import jax.numpy as jnp
from jax import lax
from jax.experimental import pallas as pl
from jax.experimental.pallas import tpu as pltpu
from jax.sharding import PartitionSpec as P

ITERATIONS = 4
HIGHEST = lax.Precision.HIGHEST
ALL = ("spec", "wave")
LANES = 128
HALF = 8
FULL = 16
PARTS = 3
CHUNK = 1024


def swap(part, mask, count):
    return lax.ppermute(part, ALL, [(i, i ^ mask) for i in range(count)])


def stages(first, count):
    found, bit = [], first
    while bit < count:
        if bit * 2 < count:
            found.append((bit, bit * 2, bit * 3))
            bit *= 4
        else:
            found.append((bit,))
            bit *= 2
    return found[::-1]


def exchange(mine, masks, count):
    others = [swap(mine, mask, count) for mask in masks]
    for other in others:
        mine = mine + other
    return mine


def dot_rows(left, right, **kwargs):
    kwargs.setdefault("preferred_element_type", jnp.float32)
    return lax.dot_general(left, right, (((1,), (1,)), ((), ())), **kwargs)


def half_parts(value):
    parts = []
    for _ in range(PARTS):
        part = value.astype(jnp.bfloat16)
        parts.append(part)
        value = value - part.astype(jnp.float32)
    return parts


def place_is_odd():
    place = lax.axis_index("spec") * lax.axis_size("wave") + lax.axis_index("wave")
    return jnp.bitwise_and(place, 1) == 1


def pad_rows(value, rows):
    blank = jnp.zeros((rows - value.shape[0], value.shape[1]), value.dtype)
    return jnp.concatenate([value, blank], axis=0)


def column_of(row):
    count = row.shape[1]
    along = lax.broadcasted_iota(jnp.int32, (count, count), 1)
    down = lax.broadcasted_iota(jnp.int32, (count, count), 0)
    return jnp.sum(jnp.where(along == down, row, 0), axis=1, keepdims=True)


def prepare_kernel(*refs):
    sources, (moved_ref, terms_ref, begun_ref), (*buffers, sems) = refs[:5], refs[5:8], refs[8:]
    copies = [
        pltpu.make_async_copy(source, buffer, sems.at[at])
        for at, (source, buffer) in enumerate(zip(sources, buffers))
    ]
    for copy in copies:
        copy.start()
    for copy in copies:
        copy.wait()
    flux_ref, offsets_ref, arch_ref, templates_ref, coefs_ref = buffers
    rows, pixels = flux_ref.shape
    own = arch_ref.shape[0]
    count, _, strip = moved_ref.shape
    pixel = lax.broadcasted_iota(jnp.int32, (rows, pixels), 1) + lax.axis_index("wave") * pixels
    flux = flux_ref[...].astype(jnp.float32)
    masked = jnp.where(pixel >= column_of(offsets_ref[...]), flux, 0.0).astype(jnp.bfloat16)
    for at in range(count):
        moved_ref[at, :rows, :] = masked[:, at * strip : (at + 1) * strip]
        moved_ref[at, rows:, :] = arch_ref[:, at * strip : (at + 1) * strip]
    parts = [pad_rows(part, FULL) for part in half_parts(templates_ref[...])]
    left = jnp.concatenate(parts, axis=0)
    grams = dot_rows(left, left)
    numer = dot_rows(parts[0], masked)
    grams = grams[:FULL] + grams[FULL : 2 * FULL] + grams[2 * FULL :]
    gram = grams[:, :FULL] + grams[:, FULL : 2 * FULL] + grams[:, 2 * FULL :]
    blank = jnp.zeros((FULL, LANES - FULL), jnp.float32)
    terms_ref[:, :LANES] = jnp.concatenate([gram, blank], axis=1)
    terms_ref[:, LANES:] = numer
    comps = templates_ref.shape[0]
    along = lax.broadcasted_iota(jnp.int32, (comps, comps), 1)
    down = lax.broadcasted_iota(jnp.int32, (comps, comps), 0)
    begun_ref[...] = dot_rows(jnp.where(along == down, 1.0, 0.0), coefs_ref[...], precision=HIGHEST)


def facts_kernel(comps, in_place, *refs):
    terms_refs, (begun_ref, ids_ref, moved_ref, out_ref) = refs[:-4], refs[-4:]
    terms = terms_refs[0][...]
    for other in terms_refs[1:]:
        terms = terms + other[...]
    begun = begun_ref[...]
    lower = jnp.dot(
        terms[:comps, :comps], begun, precision=HIGHEST, preferred_element_type=jnp.float32
    )
    first = begun * terms[:comps, LANES:] / lower
    parts = [pad_rows(part.astype(jnp.float32), FULL) for part in half_parts(first)]
    row = lax.broadcasted_iota(jnp.int32, parts[0].shape, 0)
    ids = ids_ref[...].astype(jnp.float32)
    high_ids = jnp.floor(ids * (1.0 / LANES))
    parts[0] = jnp.where(row == comps, high_ids, parts[0])
    parts[0] = jnp.where(row == comps + 1, ids - high_ids * LANES, parts[0])
    pieces = [part[at : at + HALF] for part in parts for at in (0, HALF)]
    table = jnp.concatenate(pieces, axis=1).astype(jnp.bfloat16)
    if in_place:
        sent = moved_ref.shape[1]
        out_ref[:, :sent, :] = moved_ref[...]
        for at in range(out_ref.shape[0]):
            out_ref[at, sent:, :] = table
    else:
        out_ref[...] = table


def update_basis(weights, basis, masked):
    numer = jnp.dot(weights.astype(jnp.bfloat16), masked, preferred_element_type=jnp.float32)
    cross_gram = dot_rows(weights, weights, precision=HIGHEST)
    lower = jnp.dot(cross_gram, basis, precision=HIGHEST, preferred_element_type=jnp.float32)
    return basis * numer / lower


def store_halves(mine_ref, theirs_ref, numer, gram, extra):
    comps, spectra = numer.shape
    odd = place_is_odd()
    low, high = numer[:HALF], jnp.concatenate([numer[HALF:], extra], axis=0)
    mine_ref[:, :spectra] = jnp.where(odd, high, low)
    theirs_ref[:, :spectra] = jnp.where(odd, low, high)
    wide = jnp.concatenate([gram, jnp.zeros((comps, LANES - comps), jnp.float32)], axis=1)
    wide = pad_rows(wide, FULL)
    mine_ref[:, spectra:] = jnp.where(odd, wide[HALF:], wide[:HALF])
    theirs_ref[:, spectra:] = jnp.where(odd, wide[:HALF], wide[HALF:])


def load_masked(got_ref, rows):
    count, _, strip = got_ref.shape
    return got_ref[:, :rows, :].reshape(count * rows, strip)


def load_arch(got_ref, rows, own, first, count):
    strip = got_ref.shape[2]
    arch = got_ref[pl.ds(first, count), rows : rows + own, :].astype(jnp.float32)
    arch = arch.reshape(count * own, strip)
    return arch.astype(jnp.bfloat16), (arch * arch).astype(jnp.bfloat16)


def mask_of(masked):
    return jnp.where(masked.astype(jnp.float32) != 0.0, 1.0, 0.0).astype(jnp.bfloat16)


def next_terms(basis, masked):
    return dot_rows(basis.astype(jnp.bfloat16), masked), dot_rows(basis, basis, precision=HIGHEST)


def named_hot(named_ref, arches):
    spectra = named_ref.shape[1]
    return lax.broadcasted_iota(jnp.int32, (arches, spectra), 0) == named_ref[...]


def open_kernel(rows, own, got_ref, weights_ref, basis_ref, named_ref, basis_out, mine_ref, theirs_ref):
    masked = load_masked(got_ref, rows)
    count, _, strip = got_ref.shape
    spectra = count * rows
    basis = update_basis(weights_ref[...], basis_ref[...], masked)
    basis_out[...] = basis
    numer, gram = next_terms(basis, masked)
    arch, squares = load_arch(got_ref, rows, own, 0, count)
    hot = named_hot(named_ref, count * own)
    cross = jnp.sum(jnp.where(hot, dot_rows(arch, masked), 0.0), axis=0, keepdims=True)
    normal = jnp.sum(jnp.where(hot, dot_rows(squares, mask_of(masked)), 0.0), axis=0, keepdims=True)
    power = masked.astype(jnp.float32) * masked.astype(jnp.float32)
    high = power.astype(jnp.bfloat16)
    low = (power - high.astype(jnp.float32)).astype(jnp.bfloat16)
    ones = jnp.ones((HALF, strip), jnp.bfloat16)
    energy = dot_rows(ones, high) + dot_rows(ones, low)
    blank = jnp.zeros((FULL - numer.shape[0] - 3, spectra), jnp.float32)
    extra = jnp.concatenate([cross, normal, energy[:1], blank], axis=0)
    store_halves(mine_ref, theirs_ref, numer, gram, extra)


def step_kernel(rows, last, mine_in, other_in, weights_ref, basis_ref, got_ref, weights_out, basis_out, *halves):
    odd = place_is_odd()
    comps, spectra = weights_ref.shape
    low = jnp.where(odd, other_in[...], mine_in[...])
    high = jnp.where(odd, mine_in[...], other_in[...])
    both = jnp.concatenate([low, high], axis=0)[:comps]
    gram = both[:, spectra : spectra + comps]
    weights = weights_ref[...]
    lower = jnp.dot(gram, weights, precision=HIGHEST, preferred_element_type=jnp.float32)
    weights = weights * both[:, :spectra] / lower
    weights_out[...] = weights
    masked = load_masked(got_ref, rows)
    basis = update_basis(weights, basis_ref[...], masked)
    if last:
        for at in range(basis_out.shape[0]):
            basis_out[at] = basis
        return
    basis_out[...] = basis
    numer, gram = next_terms(basis, masked)
    blank = jnp.zeros((FULL - comps, spectra), jnp.float32)
    store_halves(*halves, numer, gram, blank)


def pair_kernel(rows, own, waves, got_ref, *pair_refs):
    count, _, strip = got_ref.shape
    owners = count // waves
    masked = load_masked(got_ref, rows)
    mask = mask_of(masked)
    blank = jnp.zeros((owners * own, strip), jnp.bfloat16)
    for bits, pair_ref in enumerate(pair_refs):
        wave = jnp.bitwise_xor(lax.axis_index("wave"), bits)
        arch, squares = load_arch(got_ref, rows, own, wave * owners, owners)
        pair_ref[...] = dot_rows(masked, jnp.concatenate([arch, blank], axis=0)) + dot_rows(
            mask, jnp.concatenate([blank, squares], axis=0)
        )


def columns_of(strip):
    return [(at, min(LANES, strip - at)) for at in range(0, strip, LANES)]


def side_kernel(rows, own, at, got_ref, named_ref, mine_in, other_in, *refs):
    pair_refs, out_ref = refs[:-1], refs[-1]
    count, _, strip = got_ref.shape
    arches, spectra = count * own, count * rows
    pair = pair_refs[0][...]
    for other in pair_refs[1:]:
        pair = pair + other[...]
    out_ref[:, :rows, :] = pair.reshape(count, rows, pair.shape[1])
    table = jnp.where(place_is_odd(), mine_in[...], other_in[...])
    scale = table[at : at + 1, :spectra] / table[at + 1 : at + 2, :spectra]
    arch, _ = load_arch(got_ref, rows, own, 0, count)
    step = max(1, min(count, CHUNK // rows))
    sums = jnp.zeros((arches, strip), jnp.float32)
    counts = jnp.zeros((arches, 1), jnp.float32)
    for low in range(0, count, step):
        some = min(step, count - low)
        flux = got_ref[low : low + some, :rows, :].reshape(some * rows, strip).astype(jnp.float32)
        span = slice(low * rows, (low + some) * rows)
        hot = lax.broadcasted_iota(jnp.int32, (arches, some * rows), 0) == named_ref[:, span]
        model = 0.0
        for part in half_parts(jnp.where(hot, scale[:, span], 0.0)):
            model = model + lax.dot_general(
                part, arch, (((0,), (0,)), ((), ())), preferred_element_type=jnp.float32
            )
        residual = jnp.where(flux != 0.0, flux - model, 0.0).astype(jnp.bfloat16)
        hot = jnp.where(hot, 1.0, 0.0)
        sums = sums + jnp.dot(hot.astype(jnp.bfloat16), residual, preferred_element_type=jnp.float32)
        counts = counts + jnp.sum(hot, axis=1, keepdims=True)
    update = sums / (counts + 1.0)
    for block, (first, width) in enumerate(columns_of(strip)):
        low = rows + block * own
        out_ref[:, low : low + own, :width] = update[:, first : first + width].reshape(count, own, width)
        if width < LANES:
            out_ref[:, low : low + own, width:] = jnp.zeros((count, own, LANES - width), jnp.float32)


def close_kernel(rows, own, strip, sent_ref, energy_ref, valid_ref, chi_ref, update_ref):
    count = sent_ref.shape[0]
    share = chi_ref.shape[1]
    pair = sent_ref[0, :rows, :]
    for at in range(1, count):
        pair = pair + sent_ref[at, :rows, :]
    cross, normal = pair[:, :share], pair[:, share:]
    chi_ref[...] = (energy_ref[...] - cross * cross / normal) / valid_ref[...]
    for at in range(count):
        for block, (first, width) in enumerate(columns_of(strip)):
            low, to = rows + block * own, at * strip + first
            update_ref[:, to : to + width] = sent_ref[at, low : low + own, :width]


def line_kernel(blocks_ref, line_ref):
    count, _, strip = blocks_ref.shape
    for at in range(count):
        line_ref[:, at * strip : (at + 1) * strip] = blocks_ref[at]


def call(kernel, outs, *args, dtypes=None):
    dtypes = dtypes or [jnp.float32] * len(outs)
    in_vmem = pl.BlockSpec(memory_space=pltpu.VMEM)
    return pl.pallas_call(
        kernel,
        out_shape=[jax.ShapeDtypeStruct(shape, dtype) for shape, dtype in zip(outs, dtypes)],
        in_specs=[in_vmem] * len(args),
        out_specs=[in_vmem] * len(outs),
        compiler_params=pltpu.CompilerParams(vmem_limit_bytes=24 << 20),
    )(*args)


def on_device(spectra_flux, pixel_offsets, assignment, archetypes, coefficients, templates):
    rows, pixels = spectra_flux.shape
    own = archetypes.shape[0]
    comps = templates.shape[0]
    spec_count, wave_count = lax.axis_size("spec"), lax.axis_size("wave")
    total = spec_count * wave_count
    spectra, arches = rows * spec_count, own * spec_count
    strip = pixels // spec_count
    share = arches // wave_count
    spec_at = lax.axis_index("spec")
    table = (HALF, spectra + LANES)

    lines = 2 * PARTS * rows
    in_place = lines == strip
    fact_rows = HALF if in_place else pl.cdiv(pl.cdiv(HALF * lines, strip), HALF) * HALF
    sources = (spectra_flux, pixel_offsets[None], archetypes, templates, coefficients)
    in_vmem = pl.BlockSpec(memory_space=pltpu.VMEM)
    sent_rows = rows + own
    moved, terms, begun = pl.pallas_call(
        prepare_kernel,
        out_shape=[
            jax.ShapeDtypeStruct((spec_count, sent_rows, strip), jnp.bfloat16),
            jax.ShapeDtypeStruct((FULL, LANES + rows), jnp.float32),
            jax.ShapeDtypeStruct((comps, rows), jnp.float32),
        ],
        in_specs=[pl.BlockSpec(memory_space=pltpu.HBM)] * len(sources),
        out_specs=[in_vmem] * 3,
        scratch_shapes=[pltpu.VMEM(source.shape, source.dtype) for source in sources]
        + [pltpu.SemaphoreType.DMA((len(sources),))],
        compiler_params=pltpu.CompilerParams(vmem_limit_bytes=24 << 20),
    )(*sources)
    terms = [terms] + [swap(terms, bits, total) for bits in range(1, wave_count)]
    (facts,) = call(
        functools.partial(facts_kernel, comps, in_place),
        [(spec_count, sent_rows + HALF, strip) if in_place else (HALF, lines)],
        *(*terms, begun, assignment[None], moved),
        dtypes=[jnp.bfloat16],
    )
    if in_place:
        moved = facts
    else:
        facts = jnp.pad(facts.reshape(-1), (0, fact_rows * strip - HALF * lines))
        facts = jnp.broadcast_to(facts.reshape(1, fact_rows, strip), (spec_count, fact_rows, strip))
        moved = jnp.concatenate([moved, facts], axis=1)
    got = lax.all_to_all(moved, "spec", 0, 0, tiled=True)
    facts = got[:, rows + own :].reshape(spec_count, -1)[:, : HALF * lines].astype(jnp.float32)
    facts = facts.reshape(spec_count, HALF, PARTS, 2, rows).transpose(2, 3, 1, 0, 4)
    facts = facts.reshape(PARTS, FULL, spectra)
    weights = facts[0, :comps] + (facts[1, :comps] + facts[2, :comps])
    named = (facts[0, comps] * LANES + facts[0, comps + 1]).astype(jnp.int32)[None]

    basis = lax.dynamic_slice_in_dim(templates, spec_at * strip, strip, 1)
    basis, mine, theirs = call(
        functools.partial(open_kernel, rows, own),
        [(comps, strip), table, table],
        *(got, weights, basis, named),
    )

    first_stage, *more_stages = stages(2, total)
    mine = mine + swap(theirs, 1, total)
    mine, side_got = lax.optimization_barrier((mine, got))
    pairs = call(
        functools.partial(pair_kernel, rows, own, wave_count),
        [(spectra, 2 * share)] * wave_count,
        side_got,
    )
    mine = exchange(mine, first_stage, total)
    mine, pairs = lax.optimization_barrier((mine, pairs))
    pairs = [pairs[0]] + [swap(pairs[bits], bits, total) for bits in range(1, wave_count)]
    for masks in more_stages:
        mine = exchange(mine, masks, total)
    other = swap(mine, 1, total)
    weights, basis, next_mine, theirs = call(
        functools.partial(step_kernel, rows, False),
        [(comps, spectra), (comps, strip), table, table],
        *(mine, other, weights, basis, got),
    )
    at = comps - HALF
    energy = jnp.where(place_is_odd(), mine[at + 2], other[at + 2])
    energy = lax.dynamic_slice_in_dim(energy, spec_at * rows, rows, 0)

    first = next_mine + swap(theirs, 1, total)
    first, pairs = lax.optimization_barrier((first, pairs))
    sent_rows = rows + own * len(columns_of(strip))
    (sent,) = call(
        functools.partial(side_kernel, rows, own, at),
        [(spec_count, sent_rows, 2 * share)],
        *(got, named, mine, other, *pairs),
    )
    mine = exchange(first, first_stage, total)
    mine, sent = lax.optimization_barrier((mine, sent))
    sent = lax.all_to_all(sent, "spec", 0, 0, tiled=True)
    for iteration in range(2, ITERATIONS):
        if iteration > 2:
            mine = exchange(next_mine + swap(theirs, 1, total), first_stage, total)
        for masks in more_stages:
            mine = exchange(mine, masks, total)
        other = swap(mine, 1, total)
        last = iteration == ITERATIONS - 1
        if last:
            mine, other, sent = lax.optimization_barrier((mine, other, sent))
        outs = [(comps, spectra)]
        outs += [(spec_count, comps, strip)] if last else [(comps, strip), table, table]
        weights, basis, *halves = call(
            functools.partial(step_kernel, rows, last), outs, mine, other, weights, basis, got
        )
        if not last:
            next_mine, theirs = halves

    own_weights = lax.dynamic_slice_in_dim(weights, spec_at * rows, rows, 1)
    full = lax.all_to_all(basis, "spec", 0, 0, tiled=True)
    (full,) = call(line_kernel, [(comps, pixels)], full)
    valid = (pixels * wave_count - pixel_offsets).astype(jnp.float32)
    chi_square, update = call(
        functools.partial(close_kernel, rows, own, strip),
        [(rows, share), (own, pixels)],
        *(sent, energy[:, None], valid[:, None]),
    )
    return (chi_square, update, own_weights.T, full)


def solution(mesh):
    placed = (
        P("spec", "wave"),
        P("spec"),
        P("spec"),
        P("spec", "wave"),
        P("spec", None),
        P(None, "wave"),
    )
    return jax.shard_map(
        on_device,
        mesh=mesh,
        in_specs=placed,
        out_specs=(P("spec", "wave"), P("spec", "wave"), P("spec", None), P(None, "wave")),
        check_vma=False,
    )
```
